32 devices in a mesh: groups: 2 (over y), hid: 4 (over z), rows: 2 (over x), mp: 2 (over core).
Axes of the slice: x: 2, y: 2, z: 4, core: 2. Of those that a mesh axis runs over, the one named last changes fastest.
Arguments:
- tokens: bfloat16 [1024, 4096], P(('groups', 'rows'), 'hid'), parts along dimension 0, may hold values from -6 to 6
- norm_gain: float32 [2, 4096], P('mp'), may hold values from 0.1 to 1.9
- gate_weight: bfloat16 [2, 4096, 14336], P('mp', 'rows', 'hid'), may hold values from -0.09375 to 0.09375
- up_weight: bfloat16 [2, 4096, 14336], P('mp', 'rows', 'hid'), may hold values from -0.09375 to 0.09375
- down_weight: bfloat16 [2, 14336, 4096], P('mp', 'hid', 'rows'), may hold values from -0.046875 to 0.046875
- enc_weight: bfloat16 [2, 4096, 16384], P('mp', 'rows', 'hid'), may hold values from -0.0625 to 0.0625
- enc_bias: float32 [16384], P('hid'), may hold values from -3 to 3
- adjoint: bfloat16 [1024, 16384], P(('groups', 'rows', 'mp'), 'hid'), parts along dimension 0, may hold values from -6 to 6
Outputs:
- gated: bfloat16 [1024, 16384], P(('groups', 'rows', 'mp'), 'hid'), parts along dimension 0
The draws below stay inside these ranges and needn't reach their ends.
There are 2 independent parts, one for each index of `groups`. The reference program is written for one: setup_inputs(seed, part) draws one part's arguments, and reference() takes and returns one part's arrays. A program takes and returns all parts, laid end to end along the dimension named above; an argument that names none is the same for every part. Nothing has to cross between parts.
All inputs are finite; a program needn't handle non-finite values.
Results may differ from the reference program's by a relative error of at most 0.0058.
Values may be sent and summed in bfloat16 or wider, within the bound.
A program may use at most 128 MiB of HBM per device.

```python
import jax
import jax.numpy as jnp
from jax import lax

D = 4096
FF = 14336
FEATURES = 16384
TOKENS = 512


def levels(stream_key, dims, split, smallest, top_value):
    def one(axis_at, shards_of):
        steps = jax.random.uniform(jax.random.fold_in(jax.random.fold_in(stream_key, 6), axis_at), (shards_of,), jnp.float32, smallest / len(split), top_value / len(split))
        return jnp.repeat(jnp.exp(steps), dims[axis_at] // shards_of).reshape((-1,) + (1,) * (len(dims) - axis_at - 1))

    loudness = one(*split[0])
    for cut in split[1:]:
        loudness = loudness * one(*cut)
    return loudness


def scatter_about(key, dims, spread, reach, pieces=(), kind=jnp.bfloat16):
    values = spread * jax.random.normal(key, dims, jnp.float32)
    if pieces:
        values = values * levels(key, dims, pieces, -0.22, 0.18)
    return jnp.clip(values, -reach, reach).astype(kind)


def setup_inputs(seed: int = 0, part: int = 0) -> dict:
    splits = jax.random.split(jax.random.key(seed), 9)
    own_keys = jax.random.split(jax.random.fold_in(splits[8], part), 9)
    return {
        "tokens": scatter_about(own_keys[0], (TOKENS, D), 1.0, 6.0, ((0, 2), (1, 4))),
        "norm_gain": jnp.clip(1.0 + 0.18 * jax.random.normal(splits[1], (2, D), jnp.float32), 0.1, 1.9),
        "gate_weight": scatter_about(splits[2], (2, D, FF), D ** -0.5, 0.09375, ((0, 2), (1, 2), (2, 4))),
        "up_weight": scatter_about(splits[3], (2, D, FF), D ** -0.5, 0.09375, ((0, 2), (1, 2), (2, 4))),
        "down_weight": scatter_about(splits[4], (2, FF, D), FF ** -0.5, 0.046875, ((0, 2), (1, 4), (2, 2))),
        "enc_weight": scatter_about(splits[5], (2, D, FEATURES), (2 * D) ** -0.5, 0.0625, ((0, 2), (1, 2), (2, 4))),
        "enc_bias": scatter_about(splits[6], (FEATURES,), 0.5, 3.0, ((0, 4),), jnp.float32),
        "adjoint": scatter_about(own_keys[7], (TOKENS, FEATURES), 1.0, 6.0, ((0, 4), (1, 4))),
    }


def reference(tokens, norm_gain, gate_weight, up_weight, down_weight, enc_weight, enc_bias, adjoint):
    tokens_float = tokens.astype(jnp.float32)
    inverse_rms = lax.rsqrt(lax.optimization_barrier(jnp.mean(tokens_float * tokens_float, axis=-1, keepdims=True)) + 1e-05)
    outputs = []
    for member in range(2):
        normed = (tokens_float * inverse_rms * norm_gain[member][None, :]).astype(jnp.bfloat16)
        gate_acts = jnp.dot(normed, gate_weight[member], preferred_element_type=jnp.float32)
        up_acts = jnp.dot(normed, up_weight[member], preferred_element_type=jnp.float32)
        hidden = (jax.nn.silu(gate_acts) * up_acts).astype(jnp.bfloat16)
        outputs.append(jnp.dot(hidden, down_weight[member], preferred_element_type=jnp.float32).astype(jnp.bfloat16))
    joined = jnp.concatenate(outputs, axis=1)
    pre = jnp.dot(joined, enc_weight.reshape(2 * D, FEATURES), preferred_element_type=jnp.float32) + enc_bias[None, :]
    return (jnp.maximum(pre, 0.0) * adjoint.astype(jnp.float32)).astype(jnp.bfloat16)
```

```python
import jax
import jax.numpy as jnp
from jax import lax
from jax.sharding import PartitionSpec as P

CHUNKS = 2
BF = jnp.bfloat16
F32 = jnp.float32


def dot(a, b):
    return jnp.dot(a, b, preferred_element_type=F32)


def shift(x, axis, k):
    n = lax.axis_size(axis)
    return lax.ppermute(x, axis, [(i, (i + k) % n) for i in range(n)])


def swap(x, axis, stride):
    n = lax.axis_size(axis)
    return lax.ppermute(x, axis, [(i, i ^ stride) for i in range(n)])


def gather_doubling(x, axis, dim):
    n = lax.axis_size(axis)
    index = lax.axis_index(axis)
    stride = n // 2
    parts = [x]
    strides = []
    while stride:
        parts = parts + [swap(p, axis, stride) for p in parts]
        strides.append(stride)
        stride //= 2
    offsets = [0]
    for s in strides:
        offsets = offsets + [o ^ s for o in offsets]
    by_offset = [parts[offsets.index(o)] for o in range(n)]
    bit = 1
    while bit < n:
        flipped = (index & bit) != 0
        by_offset = [
            jnp.where(flipped, by_offset[o ^ bit], by_offset[o]) for o in range(n)
        ]
        bit *= 2
    return jnp.concatenate(by_offset, axis=dim)


def sum_over_hid(x):
    n = lax.axis_size("hid")
    index = lax.axis_index("hid")
    stride = 1
    while stride < n:
        half = x.shape[0] // 2
        bit = (index // stride) % 2
        mine = lax.dynamic_slice_in_dim(x, bit * half, half, 0)
        theirs = lax.dynamic_slice_in_dim(x, (1 - bit) * half, half, 0)
        x = mine + swap(theirs.astype(BF), "hid", stride).astype(F32)
        stride *= 2
    x = x.astype(BF)
    stride = n // 2
    while stride:
        other = swap(x, "hid", stride)
        bit = (index // stride) % 2
        low = jnp.where(bit == 0, x, other)
        high = jnp.where(bit == 0, other, x)
        x = jnp.concatenate((low, high), axis=0)
        stride //= 2
    return x


def on_device(
    tokens, norm_gain, gate_weight, up_weight, down_weight, enc_weight, enc_bias, adjoint
):
    rows, models = lax.axis_size("rows"), lax.axis_size("mp")
    row, model = lax.axis_index("rows"), lax.axis_index("mp")
    gate, up, down, enc = gate_weight[0], up_weight[0], down_weight[0], enc_weight[0]
    width = gate.shape[0]
    full = width * rows
    owned = tokens.shape[0] // models
    size = owned // CHUNKS

    tokens_float = tokens.astype(F32)
    squares = jnp.sum(tokens_float * tokens_float, axis=-1)
    stride = lax.axis_size("hid") // 2
    while stride:
        squares = squares + swap(squares, "hid", stride)
        stride //= 2
    inverse = lax.rsqrt(squares / full + 1e-05)
    inverses = [inverse] + [shift(inverse, "rows", k) for k in range(1, rows)]
    gain = lax.dynamic_slice_in_dim(norm_gain[0], row * width, width, 0)

    def columns_of(x, who):
        return lax.dynamic_slice_in_dim(x, who * width, width, 1)

    def norm_chunk(t):
        own = lax.dynamic_slice_in_dim(tokens, model * owned + t * size, size, 0)
        whole = gather_doubling(own, "hid", 1)
        blocks = [columns_of(whole, row)] + [
            shift(columns_of(whole, lax.rem(row + k, rows)), "rows", k)
            for k in range(1, rows)
        ]
        out = []
        for k in range(rows):
            stack = [blocks[k]] + [shift(blocks[k], "mp", d) for d in range(1, models)]
            scaled = []
            for d in range(models):
                who = lax.rem(model - d + models, models)
                inv = lax.dynamic_slice_in_dim(inverses[k], who * owned + t * size, size, 0)
                scaled.append((stack[d].astype(F32) * inv[:, None] * gain[None, :]).astype(BF))
            out.append(jnp.concatenate(scaled, axis=0))
        return out

    def hidden_chunk(normed):
        gates, ups = [], []
        for k in range(1, rows):
            gates.append(shift(dot(normed[k], gate).astype(BF), "rows", rows - k))
            ups.append(shift(dot(normed[k], up).astype(BF), "rows", rows - k))
        gate_acts, up_acts = dot(normed[0], gate), dot(normed[0], up)
        for g, u in zip(gates, ups):
            gate_acts = gate_acts + g.astype(F32)
            up_acts = up_acts + u.astype(F32)
        hidden = (jax.nn.silu(gate_acts) * up_acts).astype(BF)
        return [hidden] + [shift(hidden, "rows", k) for k in range(1, rows)]

    def out_chunk(hidden, t):
        block = sum_over_hid(dot(jnp.concatenate(hidden, axis=0), down))
        pre = dot(block, enc).reshape(rows, models, size, enc.shape[1])
        over_mp = pre[:, 0]
        for d in range(1, models):
            over_mp = over_mp + shift(pre[:, d].astype(BF), "mp", models - d).astype(F32)
        total = over_mp[0]
        for k in range(1, rows):
            total = total + shift(over_mp[k].astype(BF), "rows", rows - k).astype(F32)
        total = total + enc_bias[None, :]
        scale = adjoint[t * size : (t + 1) * size].astype(F32)
        return (jnp.maximum(total, 0.0) * scale).astype(BF)

    normed = [norm_chunk(t) for t in range(CHUNKS)]
    hidden = [hidden_chunk(n) for n in normed]
    outs = [out_chunk(h, t) for t, h in enumerate(hidden)]
    return jnp.concatenate(outs, axis=0)


def solution(mesh):
    placed = (
        P(("groups", "rows"), "hid"),
        P("mp", None),
        P("mp", "rows", "hid"),
        P("mp", "rows", "hid"),
        P("mp", "hid", "rows"),
        P("mp", "rows", "hid"),
        P("hid"),
        P(("groups", "rows", "mp"), "hid"),
    )
    return jax.shard_map(
        on_device,
        mesh=mesh,
        in_specs=placed,
        out_specs=P(("groups", "rows", "mp"), "hid"),
        check_vma=False,
    )
```

```python
import jax
import jax.numpy as jnp
from jax import lax
from jax.sharding import PartitionSpec as P

PIECES = (2, 2, 2, 2)
BF = jnp.bfloat16
F32 = jnp.float32


def dot(a, b):
    return jnp.dot(a, b, preferred_element_type=F32)


def shift(x, axis, k):
    n = lax.axis_size(axis)
    return lax.ppermute(x, axis, [(i, (i + k) % n) for i in range(n)])


def swap(x, axis, stride):
    n = lax.axis_size(axis)
    return lax.ppermute(x, axis, [(i, i ^ stride) for i in range(n)])


def gather_doubling(x, axis, dim):
    n = lax.axis_size(axis)
    index = lax.axis_index(axis)
    stride = n // 2
    parts = [x]
    strides = []
    while stride:
        parts = parts + [swap(p, axis, stride) for p in parts]
        strides.append(stride)
        stride //= 2
    offsets = [0]
    for s in strides:
        offsets = offsets + [o ^ s for o in offsets]
    by_offset = [parts[offsets.index(o)] for o in range(n)]
    bit = 1
    while bit < n:
        flipped = (index & bit) != 0
        by_offset = [
            jnp.where(flipped, by_offset[o ^ bit], by_offset[o]) for o in range(n)
        ]
        bit *= 2
    return jnp.concatenate(by_offset, axis=dim)


def sum_over_hid(x):
    n = lax.axis_size("hid")
    index = lax.axis_index("hid")
    stride = 1
    while stride < n:
        half = x.shape[0] // 2
        bit = (index // stride) % 2
        mine = lax.dynamic_slice_in_dim(x, bit * half, half, 0)
        theirs = lax.dynamic_slice_in_dim(x, (1 - bit) * half, half, 0)
        x = mine + swap(theirs.astype(BF), "hid", stride).astype(F32)
        stride *= 2
    x = x.astype(BF)
    stride = n // 2
    while stride:
        other = swap(x, "hid", stride)
        bit = (index // stride) % 2
        low = jnp.where(bit == 0, x, other)
        high = jnp.where(bit == 0, other, x)
        x = jnp.concatenate((low, high), axis=0)
        stride //= 2
    return x


def on_device(
    tokens, norm_gain, gate_weight, up_weight, down_weight, enc_weight, enc_bias, adjoint
):
    rows, models = lax.axis_size("rows"), lax.axis_size("mp")
    row, model = lax.axis_index("rows"), lax.axis_index("mp")
    gate, up, down, enc = gate_weight[0], up_weight[0], down_weight[0], enc_weight[0]
    width = gate.shape[0]
    full = width * rows
    owned = tokens.shape[0] // models
    sizes = [owned * p // sum(PIECES) for p in PIECES]
    starts = [sum(sizes[:t]) for t in range(len(sizes))]

    tokens_float = tokens.astype(F32)
    squares = jnp.sum(tokens_float * tokens_float, axis=-1)
    stride = lax.axis_size("hid") // 2
    while stride:
        squares = squares + swap(squares, "hid", stride)
        stride //= 2
    inverse = lax.rsqrt(squares / full + 1e-05)
    inverses = [inverse] + [shift(inverse, "rows", k) for k in range(1, rows)]
    gain = lax.dynamic_slice_in_dim(norm_gain[0], row * width, width, 0)

    def columns_of(x, who):
        return lax.dynamic_slice_in_dim(x, who * width, width, 1)

    def norm_chunk(t, after):
        size, start = sizes[t], starts[t]
        own = lax.dynamic_slice_in_dim(tokens, model * owned + start, size, 0)
        if after is not None:
            own, _ = lax.optimization_barrier((own, after))
        whole = gather_doubling(own, "hid", 1)
        blocks = [columns_of(whole, row)] + [
            shift(columns_of(whole, lax.rem(row + k, rows)), "rows", k)
            for k in range(1, rows)
        ]
        out = []
        for k in range(rows):
            stack = [blocks[k]] + [shift(blocks[k], "mp", d) for d in range(1, models)]
            scaled = []
            for d in range(models):
                who = lax.rem(model - d + models, models)
                inv = lax.dynamic_slice_in_dim(inverses[k], who * owned + start, size, 0)
                scaled.append((stack[d].astype(F32) * inv[:, None] * gain[None, :]).astype(BF))
            out.append(jnp.concatenate(scaled, axis=0))
        return out

    def project(normed):
        joined = jnp.concatenate(normed, axis=0)
        return dot(joined, gate), dot(joined, up)

    def others_of(acts):
        step = acts.shape[0] // rows
        return [acts[k * step : (k + 1) * step].astype(BF) for k in range(1, rows)]

    def send_sums(parts):
        return [shift(p, "rows", rows - k) for k, p in enumerate(parts, 1)]

    def add_up(acts, received):
        own = acts[: acts.shape[0] // rows]
        for g in received:
            own = own + g.astype(F32)
        return own

    def out_chunk(hidden, t):
        size, start = sizes[t], starts[t]
        block = sum_over_hid(dot(jnp.concatenate(hidden, axis=0), down))
        pre = dot(block, enc).reshape(rows, models, size, enc.shape[1])
        over_mp = pre[:, 0]
        for d in range(1, models):
            over_mp = over_mp + shift(pre[:, d].astype(BF), "mp", models - d).astype(F32)
        total = over_mp[0]
        for k in range(1, rows):
            total = total + shift(over_mp[k].astype(BF), "rows", rows - k).astype(F32)
        total = total + enc_bias[None, :]
        scale = adjoint[start : start + size].astype(F32)
        return (jnp.maximum(total, 0.0) * scale).astype(BF)

    outs = []
    normed = got_gate = hidden = None
    for t in range(len(sizes)):
        normed = norm_chunk(t, None if normed is None else normed[0])
        gate_acts, up_acts = project(normed)
        gate_out, up_out = others_of(gate_acts), others_of(up_acts)
        if t:
            gate_out, _ = lax.optimization_barrier((gate_out, got_gate))
            up_out, _ = lax.optimization_barrier((up_out, hidden))
        got_gate = send_sums(gate_out)
        got_up = send_sums(up_out)
        hidden = (
            jax.nn.silu(add_up(gate_acts, got_gate)) * add_up(up_acts, got_up)
        ).astype(BF)
        spread = [hidden] + [shift(hidden, "rows", k) for k in range(1, rows)]
        outs.append(out_chunk(spread, t))
    return jnp.concatenate(outs, axis=0)


def solution(mesh):
    placed = (
        P(("groups", "rows"), "hid"),
        P("mp", None),
        P("mp", "rows", "hid"),
        P("mp", "rows", "hid"),
        P("mp", "hid", "rows"),
        P("mp", "rows", "hid"),
        P("hid"),
        P(("groups", "rows", "mp"), "hid"),
    )
    return jax.shard_map(
        on_device,
        mesh=mesh,
        in_specs=placed,
        out_specs=P(("groups", "rows", "mp"), "hid"),
        check_vma=False,
    )
```

```python
import jax
import jax.numpy as jnp
from jax import lax
from jax.sharding import PartitionSpec as P

PIECES = (2, 2, 2, 2)
BF = jnp.bfloat16
F32 = jnp.float32


def dot(a, b):
    return jnp.dot(a, b, preferred_element_type=F32)


def shift(x, axis, k):
    n = lax.axis_size(axis)
    return lax.ppermute(x, axis, [(i, (i + k) % n) for i in range(n)])


def swap(x, axis, stride):
    n = lax.axis_size(axis)
    return lax.ppermute(x, axis, [(i, i ^ stride) for i in range(n)])


def gather_doubling(x, axis, dim):
    n = lax.axis_size(axis)
    index = lax.axis_index(axis)
    stride = n // 2
    parts = [x]
    strides = []
    while stride:
        parts = parts + [swap(p, axis, stride) for p in parts]
        strides.append(stride)
        stride //= 2
    offsets = [0]
    for s in strides:
        offsets = offsets + [o ^ s for o in offsets]
    by_offset = [parts[offsets.index(o)] for o in range(n)]
    bit = 1
    while bit < n:
        flipped = (index & bit) != 0
        by_offset = [
            jnp.where(flipped, by_offset[o ^ bit], by_offset[o]) for o in range(n)
        ]
        bit *= 2
    return jnp.concatenate(by_offset, axis=dim)


def sum_over_hid(x):
    n = lax.axis_size("hid")
    index = lax.axis_index("hid")
    stride = 1
    while stride < n:
        half = x.shape[0] // 2
        bit = (index // stride) % 2
        mine = lax.dynamic_slice_in_dim(x, bit * half, half, 0)
        theirs = lax.dynamic_slice_in_dim(x, (1 - bit) * half, half, 0)
        x = mine + swap(theirs.astype(BF), "hid", stride).astype(F32)
        stride *= 2
    x = x.astype(BF)
    stride = n // 2
    while stride:
        other = swap(x, "hid", stride)
        bit = (index // stride) % 2
        low = jnp.where(bit == 0, x, other)
        high = jnp.where(bit == 0, other, x)
        x = jnp.concatenate((low, high), axis=0)
        stride //= 2
    return x


def on_device(
    tokens, norm_gain, gate_weight, up_weight, down_weight, enc_weight, enc_bias, adjoint
):
    rows, models = lax.axis_size("rows"), lax.axis_size("mp")
    row, model = lax.axis_index("rows"), lax.axis_index("mp")
    gate, up, down, enc = gate_weight[0], up_weight[0], down_weight[0], enc_weight[0]
    width = gate.shape[0]
    full = width * rows
    owned = tokens.shape[0] // models
    sizes = [owned * p // sum(PIECES) for p in PIECES]
    starts = [sum(sizes[:t]) for t in range(len(sizes))]

    tokens_float = tokens.astype(F32)
    squares = jnp.sum(tokens_float * tokens_float, axis=-1)
    stride = lax.axis_size("hid") // 2
    while stride:
        squares = squares + swap(squares, "hid", stride)
        stride //= 2
    inverse = lax.rsqrt(squares / full + 1e-05)
    inverses = [inverse] + [shift(inverse, "rows", k) for k in range(1, rows)]
    gain = lax.dynamic_slice_in_dim(norm_gain[0], row * width, width, 0)

    def columns_of(x, who):
        return lax.dynamic_slice_in_dim(x, who * width, width, 1)

    def norm_all():
        own = lax.dynamic_slice_in_dim(tokens, model * owned, owned, 0)
        whole = gather_doubling(own, "hid", 1)
        blocks = [columns_of(whole, row)] + [
            shift(columns_of(whole, lax.rem(row + k, rows)), "rows", k)
            for k in range(1, rows)
        ]
        out = []
        for k in range(rows):
            stack = [blocks[k]] + [shift(blocks[k], "mp", d) for d in range(1, models)]
            scaled = []
            for d in range(models):
                who = lax.rem(model - d + models, models)
                inv = lax.dynamic_slice_in_dim(inverses[k], who * owned, owned, 0)
                scaled.append((stack[d].astype(F32) * inv[:, None] * gain[None, :]).astype(BF))
            out.append(jnp.concatenate(scaled, axis=0))
        return out

    def project(normed):
        joined = jnp.concatenate(normed, axis=0)
        return dot(joined, gate), dot(joined, up)

    def chunk_of(acts, t):
        size, start = sizes[t], starts[t]
        parts = acts.reshape(rows, models, owned, acts.shape[1])[:, :, start : start + size]
        return [parts[k].reshape(models * size, acts.shape[1]) for k in range(rows)]

    def send_sums(parts):
        return [shift(p, "rows", rows - k) for k, p in enumerate(parts, 1)]

    def add_up(acts, received):
        own = acts
        for g in received:
            own = own + g.astype(F32)
        return own

    def out_chunk(hidden, t):
        size, start = sizes[t], starts[t]
        block = sum_over_hid(dot(jnp.concatenate(hidden, axis=0), down))
        pre = dot(block, enc).reshape(rows, models, size, enc.shape[1])
        over_mp = pre[:, 0]
        for d in range(1, models):
            over_mp = over_mp + shift(pre[:, d].astype(BF), "mp", models - d).astype(F32)
        total = over_mp[0]
        for k in range(1, rows):
            total = total + shift(over_mp[k].astype(BF), "rows", rows - k).astype(F32)
        total = total + enc_bias[None, :]
        scale = adjoint[start : start + size].astype(F32)
        return (jnp.maximum(total, 0.0) * scale).astype(BF)

    outs = []
    got_gate = got_up = None
    gate_all, up_all = project(norm_all())
    for t in range(len(sizes)):
        gate_acts, up_acts = chunk_of(gate_all, t), chunk_of(up_all, t)
        gate_out = [x.astype(BF) for x in gate_acts[1:]]
        up_out = [x.astype(BF) for x in up_acts[1:]]
        if t:
            gate_out, _ = lax.optimization_barrier((gate_out, got_gate))
            up_out, _ = lax.optimization_barrier((up_out, got_up))
        got_gate = send_sums(gate_out)
        got_up = send_sums(up_out)
        hidden = (
            jax.nn.silu(add_up(gate_acts[0], got_gate)) * add_up(up_acts[0], got_up)
        ).astype(BF)
        spread = [hidden] + [shift(hidden, "rows", k) for k in range(1, rows)]
        outs.append(out_chunk(spread, t))
    return jnp.concatenate(outs, axis=0)


def solution(mesh):
    placed = (
        P(("groups", "rows"), "hid"),
        P("mp", None),
        P("mp", "rows", "hid"),
        P("mp", "rows", "hid"),
        P("mp", "hid", "rows"),
        P("mp", "rows", "hid"),
        P("hid"),
        P(("groups", "rows", "mp"), "hid"),
    )
    return jax.shard_map(
        on_device,
        mesh=mesh,
        in_specs=placed,
        out_specs=P(("groups", "rows", "mp"), "hid"),
        check_vma=False,
    )
```
